1024 devices in a mesh: section: 4 (over z_hi), expert: 32 (over z_lo, x), hidden: 8 (over y, core).
Axes of the slice: x: 4, y: 4, z: 32 (z_hi: 4, z_lo: 8; z = z_hi * 8 + z_lo), core: 2. Of those that a mesh axis runs over, the one named last changes fastest.
Arguments:
- tokens: bfloat16 [4, 512, 7168], P(None, 'expert', 'hidden'), may hold values from -12 to 12
- gate_up: bfloat16 [4, 7168, 2, 16384], P('section', 'hidden', None, 'expert'), may hold values from -0.0625 to 0.0625
- down_proj: bfloat16 [4, 16384, 7168], P('section', 'expert', 'hidden'), may hold values from -0.1875 to 0.1875
- routes: int32 [4, 4, 512, 2], P('section', None, 'expert'), may hold values from 0 to 15, all different within a row; in each aligned block of 16 rows (0 to 15, 16 to 31, ..., all dimensions but the last counted through in order) at most 3 rows name the same one
- gate_weights: bfloat16 [4, 4, 512, 2], P('section', None, 'expert'), may hold values from 0.099609375 to 0.59765625
Outputs:
- layer_outputs: bfloat16 [4, 4, 512, 7168], P('section', None, 'expert', 'hidden')
The draws below stay inside these ranges and needn't reach their ends.
Inputs may be any that keep to these rules, and one draw needn't show every extreme that they name: `routes`: in every layer and micro-batch a token names 2 different experts, and the 16 tokens of one device (aligned blocks of 16 rows) name any one expert at most 3 times; some expert is named exactly 3 times in some block.
All inputs are finite; a program needn't handle non-finite values.
Results may differ from the reference program's by a relative error of at most 0.008.
Values may be sent and summed in bfloat16 or wider, within the bound.
A program may use at most 32 MiB of HBM per device.

```python
import math
import jax
import jax.numpy as jnp
import numpy as np
from jax import lax

D = 7168
FFE = 1024
EXPERTS = 16
TOP = 2
TOK_DEV = 16
MICRO = 4
LAYERS = 4
TOKENS = 512
CAP = 3
N_EXPERT = 32


def draw_tokens(key, part):
    key_base, key_rough = jax.random.split(key, 2)
    position = jnp.arange(D, dtype=jnp.float32) / D
    feature_ramp = 0.5 * jnp.exp(position * jnp.log(3.0))
    feature_rough = jax.random.uniform(key_rough, (D,), jnp.float32, 0.6, 1.6)
    base_values = jax.random.truncated_normal(key_base, -5.0, 5.0, (MICRO, TOKENS, D), jnp.float32)
    return (base_values * feature_ramp * feature_rough).astype(jnp.bfloat16)


def block_scale(stream_key, shape, cuts, least, largest):
    def one(dim, shards_of):
        steps = jax.random.uniform(jax.random.fold_in(jax.random.fold_in(stream_key, 6), dim), (shards_of,), jnp.float32, least / len(cuts), largest / len(cuts))
        return jnp.repeat(jnp.exp(steps), shape[dim] // shards_of).reshape((-1,) + (1,) * (len(shape) - dim - 1))

    factor_of = one(*cuts[0])
    for cut in cuts[1:]:
        factor_of = factor_of * one(*cut)
    return factor_of


def assign_block(rng, own, number, rows, amount, top, most, lean):
    ranking = jax.random.permutation(rng, amount)
    heavy_load, ordinary = load_shares(amount, rows * top, most, lean, True), load_shares(amount, rows * top, most, lean, False)
    places = jnp.arange(amount)

    def named(lengths, rotation):
        used = int((lengths > 0).sum())
        fixed = max(1, used // 4)
        moved = fixed + (places - fixed + rotation * (used - fixed)) % max(1, amount - fixed)
        return jnp.zeros((amount,), jnp.int32).at[ranking[jnp.where(places < fixed, places, moved)]].set(jnp.asarray(lengths, jnp.int32))

    lengths = jnp.where(number % 4 == 0, named(heavy_load, number // 4), named(ordinary, number - number // 4 - 1))
    mixed = jax.random.permutation(jax.random.fold_in(own, 3), amount)
    source_of, sink = mixed[0:amount // 2 * 2:2], mixed[1:amount // 2 * 2:2]
    slack = jnp.minimum(lengths[source_of] - 1, most - lengths[sink]) // 2
    slack = jnp.where((source_of == ranking[0]) | (sink == ranking[0]) | (lengths[sink] == 0), 0, jnp.maximum(slack, 0))
    moved = jax.random.randint(jax.random.fold_in(own, 4), (amount // 2,), 0, 1 << 20) % (slack + 1)
    lengths = lengths.at[source_of].add(-moved).at[sink].add(moved)
    items = jnp.searchsorted(jnp.cumsum(lengths), jnp.arange(rows * top), side="right").astype(jnp.int32)
    listing = items.reshape(top, rows).T
    listing = listing[jax.random.permutation(jax.random.fold_in(own, 1), rows)]
    rotation = jax.random.randint(jax.random.fold_in(own, 2), (rows, 1), 0, top)
    return jnp.take_along_axis(listing, (jnp.arange(top)[None, :] + rotation) % top, axis=1)


def load_shares(number_of, total, reach, skew, full):
    weights = [(1 << 20) // math.isqrt(grade ** skew) + 1 for grade in range(1, number_of + 1)]
    largest = reach if full else min(reach, max(-(-total // number_of), total * weights[0] // sum(weights)))
    least = 1 if total - largest >= number_of - 1 else 0
    given, rest = [largest] + [least] * (number_of - 1), total - largest - least * (number_of - 1)
    while rest > 0:
        candidates = [i for i in range(1, number_of) if given[i] < largest] or [i for i in range(1, number_of) if given[i] < reach]
        mass, budget = sum([weights[i] for i in candidates]), rest
        for i in candidates:
            extra = min(reach - given[i], max(1, budget * weights[i] // mass), rest)
            given[i] = given[i] + extra
            rest = rest - extra
    return np.array(given)


def bell_draw(key, shape, deviation, bound, cuts=(), kind=jnp.bfloat16):
    level = block_scale(key, shape, cuts, -0.22, 0.18) if cuts else 1.0
    result = jax.random.normal(key, shape, jnp.float32) * deviation * level
    return jnp.minimum(jnp.maximum(result, -bound), bound).astype(kind)


def setup_inputs(seed: int = 0) -> dict:
    key_of = jax.random.split(jax.random.key(seed), 6)
    tokens = draw_tokens(jax.random.fold_in(key_of[5], 71), 0)
    gate_up = bell_draw(key_of[1], (LAYERS, D, 2, EXPERTS * FFE), D ** -0.5, 0.0625, ((0, 4), (1, 8), (3, 32)))
    down_proj = bell_draw(key_of[2], (LAYERS, EXPERTS * FFE, D), FFE ** -0.5, 0.1875, ((0, 4), (1, 32), (2, 8)))
    routes_keys = jax.random.split(jax.random.fold_in(key_of[3], 1), LAYERS * MICRO * TOKENS // TOK_DEV)
    routes_turns = jax.random.permutation(jax.random.fold_in(key_of[3], 3), LAYERS * MICRO * TOKENS // TOK_DEV)
    routes = jax.vmap(lambda own, number: assign_block(jax.random.fold_in(key_of[3], 2), own, number, TOK_DEV, EXPERTS, TOP, CAP, 1))(routes_keys, routes_turns).reshape((LAYERS, MICRO, TOKENS, TOP))
    gate_weights = jnp.clip(0.099609375 + 0.49804688 * jax.random.uniform(key_of[4], (LAYERS, MICRO, TOKENS, TOP), jnp.float32) ** block_scale(key_of[4], (LAYERS, MICRO, TOKENS, TOP), ((0, 4), (2, 32)), -0.2, 0.2), 0.099609375, 0.59765625).astype(jnp.bfloat16)
    return {"tokens": tokens, "gate_up": gate_up, "down_proj": down_proj, "routes": routes, "gate_weights": gate_weights}


EPS = 1e-06

def slot_tables(route_rows, gate_rows):
    expert_ids = jnp.arange(EXPERTS, dtype=jnp.int32)
    matches = route_rows[:, :, None] == expert_ids[None, None, :]
    chosen = lax.optimization_barrier(jnp.sum(matches.astype(jnp.int32), axis=1, dtype=jnp.int32))
    weight_dense = lax.optimization_barrier(jnp.sum(jnp.where(matches, gate_rows.astype(jnp.float32)[:, :, None], jnp.float32(0.0)), axis=1))
    blocked = chosen.reshape(N_EXPERT, TOK_DEV, EXPERTS)
    rank = (jnp.cumsum(blocked, axis=1, dtype=jnp.int32) - blocked).reshape(TOKENS, EXPERTS)
    source = jnp.arange(TOKENS, dtype=jnp.int32) // TOK_DEV
    slot_index = source[:, None] * CAP + rank
    return (chosen, slot_index, weight_dense)

def moe_layer(hidden_state, gate_up, down_proj, route_rows, gate_rows):
    chosen, slot_index, weight_dense = slot_tables(route_rows, gate_rows)
    slot_total = N_EXPERT * CAP
    unit_block = min(FFE, EXPERTS * FFE // N_EXPERT)
    up_table = gate_up.reshape(D, 2, EXPERTS, FFE)
    down_table = down_proj.reshape(EXPERTS, FFE, D)
    token_ids = jnp.arange(TOKENS, dtype=jnp.int32)

    def one_expert(running_sum, expert):
        column_slot = lax.dynamic_index_in_dim(slot_index, expert, 1, keepdims=False)
        column_hit = lax.dynamic_index_in_dim(chosen, expert, 1, keepdims=False)
        column_weight = lax.dynamic_index_in_dim(weight_dense, expert, 1, keepdims=False)
        target = jnp.where(column_hit == 1, column_slot, slot_total).astype(jnp.int32)
        slot_token = jnp.zeros((slot_total,), jnp.int32).at[target].set(token_ids, mode='drop')
        filled = jnp.zeros((slot_total,), jnp.float32).at[target].set(jnp.float32(1.0), mode='drop')
        slot_rows = (hidden_state[slot_token].astype(jnp.float32) * filled[:, None]).astype(jnp.bfloat16)
        slot_weight = column_weight[slot_token] * filled
        w_in = lax.dynamic_index_in_dim(up_table, expert, 2, keepdims=False).reshape(D, 2 * FFE)
        projected = jnp.dot(slot_rows, w_in, preferred_element_type=jnp.float32)
        widened = slot_rows.astype(jnp.float32)
        norm_scale = lax.rsqrt(lax.optimization_barrier(jnp.sum(widened * widened, axis=1, keepdims=True)) / D + EPS)
        activated = (jax.nn.silu(norm_scale * projected[:, :FFE]) * (norm_scale * projected[:, FFE:])).astype(jnp.bfloat16)
        w_out = lax.dynamic_index_in_dim(down_table, expert, 0, keepdims=False)
        for piece_index in range(FFE // unit_block):
            low = piece_index * unit_block
            partial_value = jnp.dot(activated[:, low:low + unit_block], w_out[low:low + unit_block], preferred_element_type=jnp.float32).astype(jnp.bfloat16)
            running_sum = running_sum.at[slot_token].add(slot_weight[:, None] * partial_value.astype(jnp.float32))
        return (running_sum, None)
    start_sum = jnp.zeros((TOKENS, D), jnp.float32)
    mixed, _ = lax.scan(one_expert, start_sum, jnp.arange(EXPERTS, dtype=jnp.int32))
    return (hidden_state.astype(jnp.float32) + mixed).astype(jnp.bfloat16)

def reference(tokens, gate_up, down_proj, routes, gate_weights):
    batch_outputs = []
    for batch_index in range(MICRO):
        hidden_state = tokens[batch_index]
        layer_list = []
        for layer_index in range(LAYERS):
            hidden_state = moe_layer(hidden_state, gate_up[layer_index], down_proj[layer_index], routes[layer_index, batch_index], gate_weights[layer_index, batch_index])
            layer_list.append(hidden_state)
        batch_outputs.append(jnp.stack(layer_list))
    return jnp.stack(batch_outputs, axis=1)
```

```python
import functools

import jax
import jax.numpy as jnp
from jax import lax
from jax.experimental import pallas as pl
from jax.experimental.pallas import tpu as pltpu
from jax.sharding import PartitionSpec as P

D = 7168
CAP = 3
PAD = 4
NX = 4
EPS = 1e-06
STAGE_TIMES = (0.0, 9.0, 13.0, 18.0, 22.0, 26.0, 36.0)
SPACING = 18.0
MESH = pl.DeviceIdType.MESH


def schedule(micro):
    steps = [
        (start + SPACING * m, m, stage) for m in range(micro) for stage, start in enumerate(STAGE_TIMES)
    ]
    return [(m, stage) for _, m, stage in sorted(steps)]


def relay_kernel(
    sizes,
    tok_ref,
    w_in_ref,
    w_out_ref,
    place_ref,
    comb_ref,
    out_ref,
    x_in,
    z_out,
    z_in,
    x_got,
    h_out,
    h_in,
    acts,
    o_rows,
    r_in,
    f_out,
    f_in,
    send_sem,
    recv_sem,
):
    ns, nz, nh, micro = sizes
    s = lax.axis_index("section")
    e = lax.axis_index("expert")
    h = lax.axis_index("hidden")
    z = e // NX
    x = e % NX
    width = w_in_ref.shape[0]
    units = w_out_ref.shape[0]
    rows = NX * nz * PAD
    chunk = rows // nh

    def z_peer(k):
        return lax.rem(z + k, nz)

    def x_peer(k):
        return lax.rem(x + k, NX)

    def h_peer(k):
        return lax.rem(h + k, nh)

    def z_dev(zz):
        return {"expert": zz * NX + x}

    def x_dev(xx):
        return {"expert": z * NX + xx}

    barrier = pltpu.get_barrier_semaphore()

    def greet(axis_device):
        pl.semaphore_signal(barrier, inc=1, device_id=axis_device, device_id_type=MESH)

    @pl.loop(1, nz)
    def _(k):
        greet(z_dev(z_peer(k)))

    @pl.loop(1, NX)
    def _(k):
        greet(x_dev(x_peer(k)))

    @pl.loop(1, nh)
    def _(k):
        greet({"hidden": h_peer(k)})

    greet({"section": lax.rem(s + 1, ns)})
    greet({"section": lax.rem(s + ns - 1, ns)})
    pl.semaphore_wait(barrier, (nz - 1) + (NX - 1) + (nh - 1) + 2)

    def send(phase, m, src, dst, device):
        pltpu.make_async_remote_copy(
            src_ref=src,
            dst_ref=dst,
            send_sem=send_sem.at[phase, m],
            recv_sem=recv_sem.at[phase, m],
            device_id=device,
            device_id_type=MESH,
        ).start()

    def wait_bytes(sem, ref):
        pltpu.make_async_copy(ref, ref, sem).wait()

    def stage_a(m):
        @pl.when(s == 0)
        def _():
            x_in[m] = tok_ref[m]

        @pl.when(s > 0)
        def _():
            wait_bytes(recv_sem.at[6, m], x_in.at[m])

        slots = jnp.dot(place_ref[m], x_in[m], preferred_element_type=jnp.float32)
        z_out[m] = slots.astype(jnp.bfloat16).reshape(2, nz, PAD, width)

        @pl.loop(1, nz)
        def _(k):
            zz = z_peer(k)
            send(0, m, z_out.at[m, :, zz], z_in.at[m, :, z], z_dev(zz))

        z_in[m, :, z] = z_out[m, :, z]

    def stage_b(m):
        wait_bytes(recv_sem.at[0, m], z_in.at[m, :, pl.ds(0, nz - 1)])

        @pl.loop(1, NX)
        def _(k):
            xx = x_peer(k)
            send(1, m, z_in.at[m, xx // 2], x_got.at[m, x], x_dev(xx))

        x_got[m, x] = z_in[m, x // 2]

    def stage_c(m):
        wait_bytes(recv_sem.at[1, m], x_got.at[m, pl.ds(0, NX - 1)])
        held = x_got[m].reshape(rows, width)
        wide = held.astype(jnp.float32)
        squares = jnp.sum(wide * wide, axis=1, keepdims=True)
        h_out[m, :, :, 2 * units :] = (
            jnp.broadcast_to(squares, (rows, 128)).astype(jnp.bfloat16).reshape(nh, chunk, 128)
        )
        h_out[m, :, :, : 2 * units] = (
            jnp.dot(held, w_in_ref[...], preferred_element_type=jnp.float32)
            .astype(jnp.bfloat16)
            .reshape(nh, chunk, 2 * units)
        )

        @pl.loop(1, nh)
        def _(k):
            hh = h_peer(k)
            send(2, m, h_out.at[m, hh], h_in.at[m, h], {"hidden": hh})

        h_in[m, h] = h_out[m, h]

    def stage_d(m):
        wait_bytes(recv_sem.at[2, m], h_in.at[m, pl.ds(0, nh - 1)])
        total = h_in[m, 0].astype(jnp.float32)
        for k in range(1, nh):
            total = total + h_in[m, k].astype(jnp.float32)
        scale = lax.rsqrt(total[:, 2 * units : 2 * units + 1] / (width * nh) + EPS)
        gate = scale * total[:, :units]
        up = scale * total[:, units : 2 * units]
        acts[m, h] = (gate / (1.0 + jnp.exp(-gate)) * up).astype(jnp.bfloat16)

        @pl.loop(1, nh)
        def _(k):
            send(3, m, acts.at[m, h], acts.at[m, h], {"hidden": h_peer(k)})

    def stage_e(m):
        wait_bytes(recv_sem.at[3, m], acts.at[m, pl.ds(0, nh - 1)])
        held = acts[m].reshape(rows, units)
        o_rows[m] = (
            jnp.dot(held, w_out_ref[...], preferred_element_type=jnp.float32)
            .astype(jnp.bfloat16)
            .reshape(NX, nz, PAD, width)
        )

        @pl.loop(1, NX)
        def _(k):
            xx = x_peer(k)
            send(4, m, o_rows.at[m, xx], r_in.at[m, x], x_dev(xx))

        r_in[m, x] = o_rows[m, x]

    def stage_f(m):
        wait_bytes(recv_sem.at[4, m], r_in.at[m, pl.ds(0, NX - 1)])
        for pair in range(2):
            both = r_in[m, 2 * pair].astype(jnp.float32) + r_in[m, 2 * pair + 1].astype(jnp.float32)
            f_out[m, pair] = both.astype(jnp.bfloat16)

        @pl.loop(1, nz)
        def _(k):
            zz = z_peer(k)
            send(5, m, f_out.at[m, :, zz], f_in.at[m, :, z], z_dev(zz))

        f_in[m, :, z] = f_out[m, :, z]

    def stage_g(m):
        wait_bytes(recv_sem.at[5, m], f_in.at[m, :, pl.ds(0, nz - 1)])
        back = f_in[m].reshape(2 * nz * PAD, width)
        mixed = jnp.dot(comb_ref[m], back, preferred_element_type=jnp.float32)
        out_ref[m] = (x_in[m].astype(jnp.float32) + mixed).astype(jnp.bfloat16)

        @pl.when(s < ns - 1)
        def _():
            send(6, m, out_ref.at[m], x_in.at[m], {"section": s + 1})

    stages = (stage_a, stage_b, stage_c, stage_d, stage_e, stage_f, stage_g)
    for m, stage in schedule(micro):
        stages[stage](m)

    for m in range(micro):
        wait_bytes(send_sem.at[0, m], z_out.at[m, :, pl.ds(0, nz - 1)])
        wait_bytes(send_sem.at[1, m], x_got.at[m, pl.ds(0, NX - 1)])
        wait_bytes(send_sem.at[2, m], h_out.at[m, pl.ds(0, nh - 1)])
        wait_bytes(send_sem.at[3, m], acts.at[m, pl.ds(0, nh - 1)])
        wait_bytes(send_sem.at[4, m], o_rows.at[m, pl.ds(0, NX - 1)])
        wait_bytes(send_sem.at[5, m], f_out.at[m, :, pl.ds(0, nz - 1)])

        @pl.when(s < ns - 1)
        def _():
            wait_bytes(send_sem.at[6, m], out_ref.at[m])


def tables(routes, gate_weights, nz):
    ids = 2 * jnp.arange(nz, dtype=jnp.int32)[None, :] + jnp.arange(2, dtype=jnp.int32)[:, None]
    ids = ids.reshape(2 * nz)
    matches = routes[:, :, :, None] == ids
    chosen = jnp.sum(matches.astype(jnp.int32), axis=2, dtype=jnp.int32)
    weight = jnp.sum(
        jnp.where(matches, gate_weights.astype(jnp.float32)[:, :, :, None], jnp.float32(0.0)), axis=2
    )
    rank = jnp.cumsum(chosen, axis=1, dtype=jnp.int32) - chosen
    caps = jnp.arange(PAD, dtype=jnp.int32)
    hits = (rank[..., None] == caps) & (chosen[..., None] == 1) & (caps < CAP)
    micro, toks = routes.shape[:2]
    hits = hits.reshape(micro, toks, 2 * nz * PAD).astype(jnp.float32)
    comb = hits * jnp.repeat(weight, PAD, axis=2)
    place = hits.transpose(0, 2, 1)
    return place.astype(jnp.bfloat16), comb.astype(jnp.bfloat16)


def on_device(tokens, gate_up, down_proj, routes, gate_weights):
    ns = lax.axis_size("section")
    nz = lax.axis_size("expert") // NX
    nh = lax.axis_size("hidden")
    micro, toks, width = tokens.shape
    units = down_proj.shape[1]
    rows = NX * nz * PAD
    chunk = rows // nh
    w_in = gate_up[0].reshape(width, 2 * units)
    w_out = down_proj[0]
    place, comb = tables(routes[0], gate_weights[0], nz)
    vmem = pl.BlockSpec(memory_space=pltpu.VMEM)
    bf16 = jnp.bfloat16
    out = pl.pallas_call(
        functools.partial(relay_kernel, (ns, nz, nh, micro)),
        out_shape=jax.ShapeDtypeStruct((micro, toks, width), bf16),
        in_specs=[vmem] * 5,
        out_specs=vmem,
        scratch_shapes=[
            pltpu.VMEM((micro, toks, width), bf16),
            pltpu.VMEM((micro, 2, nz, PAD, width), bf16),
            pltpu.VMEM((micro, 2, nz, PAD, width), bf16),
            pltpu.VMEM((micro, NX, nz, PAD, width), bf16),
            pltpu.VMEM((micro, nh, chunk, 2 * units + 128), bf16),
            pltpu.VMEM((micro, nh, chunk, 2 * units + 128), bf16),
            pltpu.VMEM((micro, nh, chunk, units), bf16),
            pltpu.VMEM((micro, NX, nz, PAD, width), bf16),
            pltpu.VMEM((micro, NX, nz, PAD, width), bf16),
            pltpu.VMEM((micro, 2, nz, PAD, width), bf16),
            pltpu.VMEM((micro, 2, nz, PAD, width), bf16),
            pltpu.SemaphoreType.DMA((7, micro)),
            pltpu.SemaphoreType.DMA((7, micro)),
        ],
        compiler_params=pltpu.CompilerParams(
            collective_id=0, has_side_effects=True, vmem_limit_bytes=40 << 20
        ),
        name="relay",
    )(tokens, w_in, w_out, place, comb)
    return out[None]


def solution(mesh):
    placed = (
        P(None, "expert", "hidden"),
        P("section", "hidden", None, "expert"),
        P("section", "expert", "hidden"),
        P("section", None, "expert", None),
        P("section", None, "expert", None),
    )
    return jax.shard_map(
        on_device,
        mesh=mesh,
        in_specs=placed,
        out_specs=P("section", None, "expert", "hidden"),
        check_vma=False,
    )
```

```python
import functools

import jax
import jax.numpy as jnp
from jax import lax
from jax.experimental import pallas as pl
from jax.experimental.pallas import tpu as pltpu
from jax.sharding import PartitionSpec as P

D = 7168
CAP = 3
PAD = 4
NX = 4
EPS = 1e-06
STAGE_TIMES = (0.0, 7.5, 12.1, 17.7, 23.1, 27.7, 35.2)
SPACING = 8.5
MESH = pl.DeviceIdType.MESH


def tables(nz, route, gate, hit_ref, comb_ref):
    toks = route.shape[0]
    slots = 2 * nz * PAD
    lane = lax.broadcasted_iota(jnp.int32, (toks, slots), 1)
    expert = 2 * (lane // PAD % nz) + lane // (PAD * nz)
    cap = lane % PAD
    first, second = route[:, 0:1] == expert, route[:, 1:2] == expert
    chosen = jnp.where(first | second, 1.0, 0.0)
    row = lax.broadcasted_iota(jnp.int32, (toks, toks), 0)
    col = lax.broadcasted_iota(jnp.int32, (toks, toks), 1)
    before = jnp.where(col < row, 1.0, 0.0).astype(jnp.bfloat16)
    rank = jnp.dot(before, chosen.astype(jnp.bfloat16), preferred_element_type=jnp.float32)
    hit = jnp.where((rank == cap.astype(jnp.float32)) & (cap < CAP), chosen, 0.0)
    wide = gate.astype(jnp.float32)
    weight = jnp.where(first, wide[:, 0:1], 0.0) + jnp.where(second, wide[:, 1:2], 0.0)
    hit_ref[...] = hit.astype(jnp.bfloat16)
    comb_ref[...] = (hit * weight).astype(jnp.bfloat16)


def schedule(micro):
    steps = [
        (start + SPACING * m, m, stage) for m in range(micro) for stage, start in enumerate(STAGE_TIMES)
    ]
    return [(m, stage) for _, m, stage in sorted(steps)]


def relay_kernel(
    sizes,
    tok_ref,
    w_in_ref,
    w_out_ref,
    route_ref,
    gate_ref,
    out_ref,
    hit_ref,
    comb_ref,
    x_in,
    z_out,
    z_in,
    x_got,
    h_out,
    h_in,
    acts,
    o_rows,
    r_in,
    f_out,
    f_in,
    send_sem,
    recv_sem,
    ready_sem,
    z_sem,
):
    ns, nz, nh, micro = sizes
    s = lax.axis_index("section")
    e = lax.axis_index("expert")
    h = lax.axis_index("hidden")
    z = e // NX
    x = e % NX
    width = w_in_ref.shape[0]
    units = w_out_ref.shape[0]
    rows = NX * nz * PAD
    chunk = rows // nh

    def z_peer(k):
        return lax.rem(z + k, nz)

    def ends(far):
        return ((z + far, z + far < nz), (z - far, z - far >= 0))

    def x_peer(k):
        return lax.rem(x + k, NX)

    def h_peer(k):
        return lax.rem(h + k, nh)

    def z_dev(zz):
        return {"expert": zz * NX + x}

    def x_dev(xx):
        return {"expert": z * NX + xx}

    barrier = pltpu.get_barrier_semaphore()

    def greet(axis_device):
        pl.semaphore_signal(barrier, inc=1, device_id=axis_device, device_id_type=MESH)

    @pl.when(s < ns - 1)
    def _():
        greet({"section": s + 1})

    @pl.loop(1, nz)
    def _(k):
        greet(z_dev(z_peer(k)))

    @pl.loop(1, NX)
    def _(k):
        greet(x_dev(x_peer(k)))

    @pl.loop(1, nh)
    def _(k):
        greet({"hidden": h_peer(k)})

    for m in range(micro):
        tables(nz, route_ref[m], gate_ref[m], hit_ref.at[m], comb_ref.at[m])
    near = (nz - 1) + (NX - 1) + (nh - 1)

    @pl.when(s == 0)
    def _():
        pl.semaphore_wait(barrier, near)

    @pl.when(s > 0)
    def _():
        pl.semaphore_wait(barrier, near + 1)
        pl.semaphore_signal(ready_sem, inc=1, device_id={"section": s - 1}, device_id_type=MESH)


    def send(phase, m, src, dst, device, arrive=None):
        pltpu.make_async_remote_copy(
            src_ref=src,
            dst_ref=dst,
            send_sem=send_sem.at[phase, m],
            recv_sem=recv_sem.at[phase, m] if arrive is None else arrive,
            device_id=device,
            device_id_type=MESH,
        ).start()

    def wait_bytes(sem, ref):
        pltpu.make_async_copy(ref, ref, sem).wait()

    def stage_a(m):
        @pl.when(s == 0)
        def _():
            x_in[m] = tok_ref[m]

        @pl.when(s > 0)
        def _():
            wait_bytes(recv_sem.at[6, m], x_in.at[m])

        slots = lax.dot_general(
            hit_ref[m], x_in[m], (((0,), (0,)), ((), ())), preferred_element_type=jnp.float32
        )
        z_out[m] = slots.astype(jnp.bfloat16).reshape(2, nz, PAD, width)

        @pl.loop(0, nz - 1)
        def _(k):
            for zz, there in ends(nz - 1 - k):
                @pl.when(there)
                def _():
                    send(0, m, z_out.at[m, :, zz], z_in.at[m, :, z], z_dev(zz), z_sem.at[m, z])

        z_in[m, :, z] = z_out[m, :, z]

    def stage_b(m):
        def forward(zz):
            @pl.loop(1, NX)
            def _(k):
                xx = x_peer(k)
                send(1, m, z_in.at[m, xx // 2, zz], x_got.at[m, x, zz], x_dev(xx))

        forward(z)

        @pl.loop(1, nz)
        def _(far):
            for zz, there in ends(far):

                @pl.when(there)
                def _():
                    wait_bytes(z_sem.at[m, zz], z_in.at[m, :, 0])
                    forward(zz)

        x_got[m, x] = z_in[m, x // 2]

    def stage_c(m):
        wait_bytes(recv_sem.at[1, m], x_got.at[m, pl.ds(0, NX - 1)])
        held = x_got[m].reshape(rows, width)
        wide = held.astype(jnp.float32)
        squares = jnp.sum(wide * wide, axis=1, keepdims=True)
        h_out[m, :, :, 2 * units :] = (
            jnp.broadcast_to(squares, (rows, 128)).astype(jnp.bfloat16).reshape(nh, chunk, 128)
        )
        h_out[m, :, :, : 2 * units] = (
            jnp.dot(held, w_in_ref[...], preferred_element_type=jnp.float32)
            .astype(jnp.bfloat16)
            .reshape(nh, chunk, 2 * units)
        )

        @pl.loop(1, nh)
        def _(k):
            hh = h_peer(k)
            send(2, m, h_out.at[m, hh], h_in.at[m, h], {"hidden": hh})

        h_in[m, h] = h_out[m, h]

    def stage_d(m):
        wait_bytes(recv_sem.at[2, m], h_in.at[m, pl.ds(0, nh - 1)])
        total = h_in[m, 0].astype(jnp.float32)
        for k in range(1, nh):
            total = total + h_in[m, k].astype(jnp.float32)
        scale = lax.rsqrt(total[:, 2 * units : 2 * units + 1] / (width * nh) + EPS)
        gate = scale * total[:, :units]
        up = scale * total[:, units : 2 * units]
        acts[m, h] = (gate / (1.0 + jnp.exp(-gate)) * up).astype(jnp.bfloat16)

        @pl.loop(1, nh)
        def _(k):
            send(3, m, acts.at[m, h], acts.at[m, h], {"hidden": h_peer(k)})

    def stage_e(m):
        wait_bytes(recv_sem.at[3, m], acts.at[m, pl.ds(0, nh - 1)])
        held = acts[m].reshape(rows, units)
        o_rows[m] = (
            jnp.dot(held, w_out_ref[...], preferred_element_type=jnp.float32)
            .astype(jnp.bfloat16)
            .reshape(NX, nz, PAD, width)
        )

        @pl.loop(1, NX)
        def _(k):
            xx = x_peer(k)
            send(4, m, o_rows.at[m, xx], r_in.at[m, x], x_dev(xx))

        r_in[m, x] = o_rows[m, x]

    def stage_f(m):
        wait_bytes(recv_sem.at[4, m], r_in.at[m, pl.ds(0, NX - 1)])
        for pair in range(2):
            both = r_in[m, 2 * pair].astype(jnp.float32) + r_in[m, 2 * pair + 1].astype(jnp.float32)
            f_out[m, pair] = both.astype(jnp.bfloat16)

        @pl.loop(0, nz - 1)
        def _(k):
            for zz, there in ends(nz - 1 - k):
                @pl.when(there)
                def _():
                    send(5, m, f_out.at[m, :, zz], f_in.at[m, :, z], z_dev(zz))

        f_in[m, :, z] = f_out[m, :, z]

    def stage_g(m):
        wait_bytes(recv_sem.at[5, m], f_in.at[m, :, pl.ds(0, nz - 1)])
        back = f_in[m].reshape(2 * nz * PAD, width)
        mixed = jnp.dot(comb_ref[m], back, preferred_element_type=jnp.float32)
        out_ref[m] = (x_in[m].astype(jnp.float32) + mixed).astype(jnp.bfloat16)

        @pl.when(s < ns - 1)
        def _():
            if m == 0:
                pl.semaphore_wait(ready_sem, 1)
            send(6, m, out_ref.at[m], x_in.at[m], {"section": s + 1})

    stages = (stage_a, stage_b, stage_c, stage_d, stage_e, stage_f, stage_g)
    for m, stage in schedule(micro):
        stages[stage](m)

    for m in range(micro):
        wait_bytes(send_sem.at[0, m], z_out.at[m, :, pl.ds(0, nz - 1)])
        wait_bytes(send_sem.at[1, m], x_got.at[m, pl.ds(0, NX - 1)])
        wait_bytes(send_sem.at[2, m], h_out.at[m, pl.ds(0, nh - 1)])
        wait_bytes(send_sem.at[3, m], acts.at[m, pl.ds(0, nh - 1)])
        wait_bytes(send_sem.at[4, m], o_rows.at[m, pl.ds(0, NX - 1)])
        wait_bytes(send_sem.at[5, m], f_out.at[m, :, pl.ds(0, nz - 1)])

        @pl.when(s < ns - 1)
        def _():
            wait_bytes(send_sem.at[6, m], out_ref.at[m])


def on_device(tokens, gate_up, down_proj, routes, gate_weights):
    ns = lax.axis_size("section")
    nz = lax.axis_size("expert") // NX
    nh = lax.axis_size("hidden")
    micro, toks, width = tokens.shape
    units = down_proj.shape[1]
    rows = NX * nz * PAD
    chunk = rows // nh
    w_in = gate_up[0].reshape(width, 2 * units)
    w_out = down_proj[0]
    vmem = pl.BlockSpec(memory_space=pltpu.VMEM)
    bf16 = jnp.bfloat16
    out = pl.pallas_call(
        functools.partial(relay_kernel, (ns, nz, nh, micro)),
        out_shape=jax.ShapeDtypeStruct((micro, toks, width), bf16),
        in_specs=[vmem] * 5,
        out_specs=vmem,
        scratch_shapes=[
            pltpu.VMEM((micro, toks, 2 * nz * PAD), bf16),
            pltpu.VMEM((micro, toks, 2 * nz * PAD), bf16),
            pltpu.VMEM((micro, toks, width), bf16),
            pltpu.VMEM((micro, 2, nz, PAD, width), bf16),
            pltpu.VMEM((micro, 2, nz, PAD, width), bf16),
            pltpu.VMEM((micro, NX, nz, PAD, width), bf16),
            pltpu.VMEM((micro, nh, chunk, 2 * units + 128), bf16),
            pltpu.VMEM((micro, nh, chunk, 2 * units + 128), bf16),
            pltpu.VMEM((micro, nh, chunk, units), bf16),
            pltpu.VMEM((micro, NX, nz, PAD, width), bf16),
            pltpu.VMEM((micro, NX, nz, PAD, width), bf16),
            pltpu.VMEM((micro, 2, nz, PAD, width), bf16),
            pltpu.VMEM((micro, 2, nz, PAD, width), bf16),
            pltpu.SemaphoreType.DMA((7, micro)),
            pltpu.SemaphoreType.DMA((7, micro)),
            pltpu.SemaphoreType.REGULAR,
            pltpu.SemaphoreType.DMA((micro, nz)),
        ],
        compiler_params=pltpu.CompilerParams(
            collective_id=0, has_side_effects=True, vmem_limit_bytes=40 << 20
        ),
        name="relay",
    )(tokens, w_in, w_out, routes[0], gate_weights[0])
    return out[None]


def solution(mesh):
    placed = (
        P(None, "expert", "hidden"),
        P("section", "hidden", None, "expert"),
        P("section", "expert", "hidden"),
        P("section", None, "expert", None),
        P("section", None, "expert", None),
    )
    return jax.shard_map(
        on_device,
        mesh=mesh,
        in_specs=placed,
        out_specs=P("section", None, "expert", "hidden"),
        check_vma=False,
    )
```

```python
import functools

import jax
import jax.numpy as jnp
from jax import lax
from jax.experimental import pallas as pl
from jax.experimental.pallas import tpu as pltpu
from jax.sharding import PartitionSpec as P

D = 7168
CAP = 3
PAD = 4
NX = 4
EPS = 1e-06
ORDER = (
    0, 1, 10, 2, 3, 11, 4, 20,
    12, 5, 13, 6, 21, 14, 30, 22,
    15, 7, 23, 16, 31, 24, 32, 25,
    17, 33, 26, 34, 35, 27, 36, 37,
)
MESH = pl.DeviceIdType.MESH


def tables(nz, route, gate, hit_ref, comb_ref):
    toks = route.shape[0]
    slots = 2 * nz * CAP
    lane = lax.broadcasted_iota(jnp.int32, (toks, slots), 1)
    expert = 2 * (lane // (2 * CAP)) + lane % 2
    cap = lane % (2 * CAP) // 2
    first, second = route[:, 0:1] == expert, route[:, 1:2] == expert
    chosen = jnp.where(first | second, 1.0, 0.0)
    row = lax.broadcasted_iota(jnp.int32, (toks, toks), 0)
    col = lax.broadcasted_iota(jnp.int32, (toks, toks), 1)
    before = jnp.where(col < row, 1.0, 0.0).astype(jnp.bfloat16)
    rank = jnp.dot(before, chosen.astype(jnp.bfloat16), preferred_element_type=jnp.float32)
    hit = jnp.where(rank == cap.astype(jnp.float32), chosen, 0.0)
    wide = gate.astype(jnp.float32)
    weight = jnp.where(first, wide[:, 0:1], 0.0) + jnp.where(second, wide[:, 1:2], 0.0)
    hit_ref[...] = hit.astype(jnp.bfloat16)
    comb_ref[...] = (hit * weight).astype(jnp.bfloat16)


def regroupings(nz, to_x_ref, to_z_ref):
    slots, group = 2 * nz * CAP, nz * CAP
    r = lax.broadcasted_iota(jnp.int32, (slots, slots), 0)
    j = lax.broadcasted_iota(jnp.int32, (slots, slots), 1)
    source = 2 * (r % group) + r // group
    to_x_ref[...] = jnp.where(source == j, 1.0, 0.0).astype(jnp.bfloat16)
    r = lax.broadcasted_iota(jnp.int32, (slots, NX * group), 1)
    j = lax.broadcasted_iota(jnp.int32, (slots, NX * group), 0)
    target = 2 * (r % group) + r // (2 * group)
    to_z_ref[...] = jnp.where(target == j, 1.0, 0.0).astype(jnp.bfloat16)


def relay_kernel(
    sizes,
    tok_ref,
    w_in_ref,
    w_out_ref,
    route_ref,
    gate_ref,
    out_ref,
    hit_ref,
    comb_ref,
    to_x_ref,
    to_z_ref,
    x_in,
    z_out,
    z_in,
    x_out,
    x_got,
    p_out,
    p_in,
    y_out,
    y_in,
    acts,
    o_rows,
    r_in,
    f_out,
    f_in,
    send_sem,
    recv_sem,
    ready_sem,
):
    ns, nz, nh, micro = sizes
    ny = nh // 2
    s = lax.axis_index("section")
    e = lax.axis_index("expert")
    h = lax.axis_index("hidden")
    z = e // NX
    x = e % NX
    y = h // 2
    core = h % 2
    width = w_in_ref.shape[0]
    units = w_out_ref.shape[0]
    half = units // 2
    slots = 2 * nz * CAP
    group = nz * CAP
    rows = NX * group
    chunk = rows // ny

    def ends(far):
        return ((z + far, z + far < nz), (z - far, z - far >= 0))

    def x_peer(k):
        return lax.rem(x + k, NX)

    def y_peer(k):
        return lax.rem(y + k, ny)

    def h_peer(k):
        return lax.rem(h + k, nh)

    def z_dev(zz):
        return {"expert": zz * NX + x}

    def x_dev(xx):
        return {"expert": z * NX + xx}

    barrier = pltpu.get_barrier_semaphore()

    def greet(axis_device):
        pl.semaphore_signal(barrier, inc=1, device_id=axis_device, device_id_type=MESH)

    @pl.when(s < ns - 1)
    def _():
        greet({"section": s + 1})

    @pl.loop(1, nz)
    def _(k):
        greet(z_dev(lax.rem(z + k, nz)))

    @pl.loop(1, NX)
    def _(k):
        greet(x_dev(x_peer(k)))

    @pl.loop(1, nh)
    def _(k):
        greet({"hidden": h_peer(k)})

    for m in range(micro):
        tables(nz, route_ref[m], gate_ref[m], hit_ref.at[m], comb_ref.at[m])
    regroupings(nz, to_x_ref, to_z_ref)
    near = (nz - 1) + (NX - 1) + (nh - 1)

    @pl.when(s == 0)
    def _():
        pl.semaphore_wait(barrier, near)

    @pl.when(s > 0)
    def _():
        pl.semaphore_wait(barrier, near + 1)
        pl.semaphore_signal(ready_sem, inc=1, device_id={"section": s - 1}, device_id_type=MESH)

    def send(phase, m, src, dst, device):
        pltpu.make_async_remote_copy(
            src_ref=src,
            dst_ref=dst,
            send_sem=send_sem.at[phase, m],
            recv_sem=recv_sem.at[phase, m],
            device_id=device,
            device_id_type=MESH,
        ).start()

    def wait_bytes(sem, ref):
        pltpu.make_async_copy(ref, ref, sem).wait()

    def matmul(a, b):
        return jnp.dot(a, b, preferred_element_type=jnp.float32)

    def stage_a(m):
        @pl.when(s == 0)
        def _():
            x_in[m] = tok_ref[m]

        @pl.when(s > 0)
        def _():
            wait_bytes(recv_sem.at[7, m], x_in.at[m])

        picked = lax.dot_general(
            hit_ref[m], x_in[m], (((0,), (0,)), ((), ())), preferred_element_type=jnp.float32
        )
        z_out[m] = picked.astype(jnp.bfloat16).reshape(nz, CAP, 2, width)

        @pl.loop(0, nz - 1)
        def _(k):
            for zz, there in ends(nz - 1 - k):

                @pl.when(there)
                def _():
                    send(0, m, z_out.at[m, zz], z_in.at[m, z], z_dev(zz))

        z_in[m, z] = z_out[m, z]

    def stage_b(m):
        wait_bytes(recv_sem.at[0, m], z_in.at[m, pl.ds(0, nz - 1)])
        sorted_rows = matmul(to_x_ref[...], z_in[m].reshape(slots, width))
        x_out[m] = sorted_rows.astype(jnp.bfloat16).reshape(2, group, width)

        @pl.loop(1, NX)
        def _(k):
            xx = x_peer(k)
            send(1, m, x_out.at[m, xx // 2], x_got.at[m, x], x_dev(xx))

        x_got[m, x] = x_out[m, x // 2]

    def stage_c(m):
        wait_bytes(recv_sem.at[1, m], x_got.at[m, pl.ds(0, NX - 1)])
        held = x_got[m].reshape(rows, width)
        projected = matmul(held, w_in_ref[...]).astype(jnp.bfloat16)
        wide = held.astype(jnp.float32)
        squares = jnp.sum(wide * wide, axis=1, keepdims=True)
        spread = jnp.broadcast_to(squares, (rows, 128)).astype(jnp.bfloat16)
        for c in range(2):
            p_out[m, c, :, :half] = projected[:, c * half : (c + 1) * half]
            p_out[m, c, :, half:units] = projected[:, units + c * half : units + (c + 1) * half]
            p_out[m, c, :, units:] = spread
        send(2, m, p_out.at[m, 1 - core], p_in.at[m], {"hidden": 2 * y + 1 - core})

    def stage_d(m):
        wait_bytes(recv_sem.at[2, m], p_in.at[m])
        both = p_out[m, core].astype(jnp.float32) + p_in[m].astype(jnp.float32)
        y_out[m] = both.astype(jnp.bfloat16).reshape(ny, chunk, units + 128)

        @pl.loop(1, ny)
        def _(k):
            yy = y_peer(k)
            send(3, m, y_out.at[m, yy], y_in.at[m, y], {"hidden": 2 * yy + core})

        y_in[m, y] = y_out[m, y]

    def stage_e(m):
        wait_bytes(recv_sem.at[3, m], y_in.at[m, pl.ds(0, ny - 1)])
        total = y_in[m, 0].astype(jnp.float32)
        for k in range(1, ny):
            total = total + y_in[m, k].astype(jnp.float32)
        scale = lax.rsqrt(total[:, units : units + 1] / (width * nh) + EPS)
        gate = scale * total[:, :half]
        up = scale * total[:, half:units]
        mine = core * ny + y
        acts[m, mine] = (gate / (1.0 + jnp.exp(-gate)) * up).astype(jnp.bfloat16)

        @pl.loop(1, nh)
        def _(k):
            send(4, m, acts.at[m, mine], acts.at[m, mine], {"hidden": h_peer(k)})

    def stage_f(m):
        wait_bytes(recv_sem.at[4, m], acts.at[m, pl.ds(0, nh - 1)])
        low = acts[m, :ny].reshape(rows, half)
        high = acts[m, ny:].reshape(rows, half)
        made = matmul(low, w_out_ref[:half]) + matmul(high, w_out_ref[half:])
        o_rows[m] = made.astype(jnp.bfloat16).reshape(NX, group, width)

        @pl.loop(1, NX)
        def _(k):
            xx = x_peer(k)
            send(5, m, o_rows.at[m, xx], r_in.at[m, x], x_dev(xx))

        r_in[m, x] = o_rows[m, x]

    def stage_g(m):
        wait_bytes(recv_sem.at[5, m], r_in.at[m, pl.ds(0, NX - 1)])
        paired = matmul(to_z_ref[...], r_in[m].reshape(rows, width))
        f_out[m] = paired.astype(jnp.bfloat16).reshape(nz, CAP, 2, width)

        @pl.loop(0, nz - 1)
        def _(k):
            for zz, there in ends(nz - 1 - k):

                @pl.when(there)
                def _():
                    send(6, m, f_out.at[m, zz], f_in.at[m, z], z_dev(zz))

        f_in[m, z] = f_out[m, z]

    def stage_h(m):
        wait_bytes(recv_sem.at[6, m], f_in.at[m, pl.ds(0, nz - 1)])
        mixed = matmul(comb_ref[m], f_in[m].reshape(slots, width))
        out_ref[m] = (x_in[m].astype(jnp.float32) + mixed).astype(jnp.bfloat16)

        @pl.when(s < ns - 1)
        def _():
            if m == 0:
                pl.semaphore_wait(ready_sem, 1)
            send(7, m, out_ref.at[m], x_in.at[m], {"section": s + 1})

    stages = (stage_a, stage_b, stage_c, stage_d, stage_e, stage_f, stage_g, stage_h)
    for step in ORDER:
        m, stage = step // 10, step % 10
        if m < micro:
            stages[stage](m)

    for m in range(micro):
        wait_bytes(send_sem.at[0, m], z_out.at[m, pl.ds(0, nz - 1)])
        wait_bytes(send_sem.at[1, m], x_got.at[m, pl.ds(0, NX - 1)])
        wait_bytes(send_sem.at[2, m], p_in.at[m])
        wait_bytes(send_sem.at[3, m], y_out.at[m, pl.ds(0, ny - 1)])
        wait_bytes(send_sem.at[4, m], acts.at[m, pl.ds(0, nh - 1)])
        wait_bytes(send_sem.at[5, m], o_rows.at[m, pl.ds(0, NX - 1)])
        wait_bytes(send_sem.at[6, m], f_out.at[m, pl.ds(0, nz - 1)])

        @pl.when(s < ns - 1)
        def _():
            wait_bytes(send_sem.at[7, m], out_ref.at[m])


def on_device(tokens, gate_up, down_proj, routes, gate_weights):
    ns = lax.axis_size("section")
    nz = lax.axis_size("expert") // NX
    nh = lax.axis_size("hidden")
    ny = nh // 2
    micro, toks, width = tokens.shape
    units = down_proj.shape[1]
    slots, group = 2 * nz * CAP, nz * CAP
    rows = NX * group
    chunk = rows // ny
    w_in = gate_up[0].reshape(width, 2 * units)
    w_out = down_proj[0]
    vmem = pl.BlockSpec(memory_space=pltpu.VMEM)
    bf16 = jnp.bfloat16

    def held(*shape):
        return pltpu.VMEM((micro, *shape), bf16)

    out = pl.pallas_call(
        functools.partial(relay_kernel, (ns, nz, nh, micro)),
        out_shape=jax.ShapeDtypeStruct((micro, toks, width), bf16),
        in_specs=[vmem] * 5,
        out_specs=vmem,
        scratch_shapes=[
            held(toks, slots),
            held(toks, slots),
            pltpu.VMEM((slots, slots), bf16),
            pltpu.VMEM((slots, rows), bf16),
            held(toks, width),
            held(nz, CAP, 2, width),
            held(nz, CAP, 2, width),
            held(2, group, width),
            held(NX, group, width),
            held(2, rows, units + 128),
            held(rows, units + 128),
            held(ny, chunk, units + 128),
            held(ny, chunk, units + 128),
            held(nh, chunk, units // 2),
            held(NX, group, width),
            held(NX, group, width),
            held(nz, CAP, 2, width),
            held(nz, CAP, 2, width),
            pltpu.SemaphoreType.DMA((8, micro)),
            pltpu.SemaphoreType.DMA((8, micro)),
            pltpu.SemaphoreType.REGULAR,
        ],
        compiler_params=pltpu.CompilerParams(
            collective_id=0, has_side_effects=True, vmem_limit_bytes=40 << 20
        ),
        name="relay",
    )(tokens, w_in, w_out, routes[0], gate_weights[0])
    return out[None]


def solution(mesh):
    placed = (
        P(None, "expert", "hidden"),
        P("section", "hidden", None, "expert"),
        P("section", "expert", "hidden"),
        P("section", None, "expert", None),
        P("section", None, "expert", None),
    )
    return jax.shard_map(
        on_device,
        mesh=mesh,
        in_specs=placed,
        out_specs=P("section", None, "expert", "hidden"),
        check_vma=False,
    )
```
